32 devices in a mesh: dp: 2 (over x), ctx: 16 (over z, y, core).
Axes of the slice: x: 2, y: 2, z: 4, core: 2. Of those that a mesh axis runs over, the one named last changes fastest.
Arguments:
- features: bfloat16 [2, 2048, 1024], P('dp', 'ctx'), may hold values from -6 to 6
- gate_in: bfloat16 [2, 2048, 1024], P('dp', 'ctx'), may hold values from -6 to 6
- state_in: bfloat16 [2, 2048, 64], P('dp', 'ctx'), may hold values from -0.59765625 to 0.59765625
- state_out: bfloat16 [2, 2048, 64], P('dp', 'ctx'), may hold values from -0.59765625 to 0.59765625
- step_size: float32 [2, 8, 2048], P('dp', None, 'ctx'), may hold values from 0 to 4096
- decay_rate: float32 [8], replicated, may hold values from 0 to 1
- user_ids: int32 [2, 2048], P('dp', 'ctx'), may hold values from 0 to 3, never falling along the last dimension, each value on 1 to 1024 neighbouring positions
- norm_gain: bfloat16 [1024], replicated, may hold values from 0.099609375 to 1.8984375
- out_weight: bfloat16 [1024, 512], P(('dp', 'ctx')), may hold values from -0.1875 to 0.1875
- out_grad: bfloat16 [2, 2048, 512], P('dp', 'ctx'), may hold values from -6 to 6
Outputs:
- mixed: bfloat16 [2, 2048, 512], P('dp', 'ctx')
- feature_grad: bfloat16 [2, 2048, 1024], P('dp', 'ctx')
- weight_grad: float32 [1024, 512], P(('dp', 'ctx'))
The draws below stay inside these ranges and needn't reach their ends.
Inputs may be any that keep to these rules, and one draw needn't show every extreme that they name: `user_ids`: each of the 4 users of a history holds consecutive events; ids never fall along a history, and one user holds exactly 1024 events.
All inputs are finite; a program needn't handle non-finite values.
Results may differ from the reference program's by a relative error of at most 0.019.
Values may be sent and summed in bfloat16 or wider, within the bound.
A program may use at most 64 MiB of HBM per device.

```python
import math
import jax
import jax.numpy as jnp
import numpy as np
from jax import lax

DW = 512
HEADS = 8
NSTATE = 64
TOK_DEV = 128
INNER = 1024
PACKED_OCCASIONS = 2048
USERS = 4
N_DP = 2


def draw_step_size(key, part):
    identifier_seed, segment_lookup_entries, identifier_offset, spurt_identifier = jax.random.split(key, 4)
    entire_dimensions = (N_DP, HEADS, PACKED_OCCASIONS)
    baseline_tolerance = jnp.exp(jax.random.uniform(identifier_seed, entire_dimensions, jnp.float32, math.log(0.5), math.log(2.0)))
    block_scale = jnp.exp(jax.random.uniform(segment_lookup_entries, (N_DP, 1, PACKED_OCCASIONS // TOK_DEV), jnp.float32, math.log(0.4), math.log(2.5)))
    multiplier_value = jnp.repeat(block_scale, TOK_DEV, axis=2)
    spurt_offset = jax.random.randint(identifier_offset, (N_DP, 4, 1), 0, PACKED_OCCASIONS)
    token_offsets = jnp.arange(PACKED_OCCASIONS, dtype=jnp.int32)
    spurt_enabled = jnp.any(token_offsets[None, None, :] == spurt_offset, axis=1)[:, None, :]
    spurt_length = PACKED_OCCASIONS * jax.random.uniform(spurt_identifier, entire_dimensions, jnp.float32, 0.8, 2.0)
    return jnp.where(spurt_enabled, spurt_length, baseline_tolerance * multiplier_value)


def draw_decay_rate(key, part):
    key_order, key_slow, key_fast = jax.random.split(key, 3)
    ranking = jax.random.permutation(key_order, HEADS)
    forgetful = ranking < HEADS // 2
    slow_rate = jnp.exp(jax.random.uniform(key_slow, (HEADS,), jnp.float32, math.log(0.1), math.log(0.3))) / PACKED_OCCASIONS
    fast_rate = jnp.exp(jax.random.uniform(key_fast, (HEADS,), jnp.float32, math.log(0.015), math.log(0.04)))
    return jnp.where(forgetful, fast_rate, slow_rate)


def level_of(own_key, extent, cuts, low, top_value):
    def one(position, blocks):
        heights = jax.random.uniform(jax.random.fold_in(jax.random.fold_in(own_key, 6), position), (blocks,), jnp.float32, low / len(cuts), top_value / len(cuts))
        return jnp.repeat(jnp.exp(heights), extent[position] // blocks).reshape((-1,) + (1,) * (len(extent) - position - 1))

    factor_of = one(*cuts[0])
    for cut in cuts[1:]:
        factor_of = factor_of * one(*cut)
    return factor_of


def length_profile(number_of, total, most, skew):
    weights = [(1 << 20) // math.isqrt(rank ** skew) + 1 for rank in range(2, number_of + 1)]
    surplus, counts = total - most - (number_of - 1), [1] * (number_of - 1)
    while surplus > 0:
        candidates = [i for i in range(number_of - 1) if counts[i] < most]
        whole, budget = sum([weights[i] for i in candidates]), surplus
        for i in candidates:
            extra = min(most - counts[i], max(1, budget * weights[i] // whole), surplus)
            counts[i] = counts[i] + extra
            surplus = surplus - extra
    return np.array([most] + counts)


def uneven_parts(stream_key, count, total, reach, skew):
    if count == 2:
        one = jax.random.randint(stream_key, (), max(1, total - reach), min(reach, total - 1) + 1)
        return jnp.stack([one, total - one])
    lengths = jnp.asarray(length_profile(count, total, reach, skew), jnp.int32)
    twos = (count - 1) // 2
    donor, sink = lengths[1:1 + 2 * twos:2], lengths[2:2 + 2 * twos:2]
    slack = jnp.minimum(donor - 1, reach - sink)
    passed = jax.random.randint(jax.random.fold_in(stream_key, 1), (twos,), 0, 1 << 20) % (slack + 1)
    lengths = lengths.at[1:1 + 2 * twos:2].set(donor - passed).at[2:2 + 2 * twos:2].set(sink + passed)
    return lengths[jax.random.permutation(jax.random.fold_in(stream_key, 2), count)]


def centred(own_key, extent, scale, most, shards=(), kind=jnp.bfloat16):
    array = jax.random.normal(own_key, extent, jnp.float32) * scale
    if len(shards) > 0:
        array = level_of(own_key, extent, shards, -0.22, 0.18) * array
    return jnp.clip(array, min=-most, max=most).astype(kind)


def setup_inputs(seed: int = 0) -> dict:
    arg_keys = jax.random.split(jax.random.key(seed), 11)
    features = centred(arg_keys[0], (N_DP, PACKED_OCCASIONS, INNER), 1.0, 6.0, ((0, 2), (1, 16)))
    gate_in = centred(arg_keys[1], (N_DP, PACKED_OCCASIONS, INNER), 1.0, 6.0, ((0, 2), (1, 16)))
    state_in = centred(arg_keys[2], (N_DP, PACKED_OCCASIONS, NSTATE), 0.1, 0.59765625, ((0, 2), (1, 16)))
    state_out = centred(arg_keys[3], (N_DP, PACKED_OCCASIONS, NSTATE), 0.1, 0.59765625, ((0, 2), (1, 16)))
    step_size = draw_step_size(jax.random.fold_in(arg_keys[10], 71), 0)
    decay_rate = draw_decay_rate(jax.random.fold_in(arg_keys[10], 71), 0)
    user_ids = jax.vmap(lambda own: jnp.searchsorted(jnp.cumsum(uneven_parts(own, USERS, PACKED_OCCASIONS, PACKED_OCCASIONS // 2, 2)), jnp.arange(PACKED_OCCASIONS), side="right"))(jax.random.split(arg_keys[6], N_DP)).reshape((N_DP, PACKED_OCCASIONS)).astype(jnp.int32)
    norm_gain = jnp.clip(1.0 + 0.18 * jax.random.normal(arg_keys[7], (INNER,), jnp.float32), 0.099609375, 1.8984375).astype(jnp.bfloat16)
    out_weight = centred(arg_keys[8], (INNER, DW), INNER ** -0.5, 0.1875, ((0, 32),))
    out_grad = centred(arg_keys[9], (N_DP, PACKED_OCCASIONS, DW), 1.0, 6.0, ((0, 2), (1, 16)))
    return {"features": features, "gate_in": gate_in, "state_in": state_in, "state_out": state_out, "step_size": step_size, "decay_rate": decay_rate, "user_ids": user_ids, "norm_gain": norm_gain, "out_weight": out_weight, "out_grad": out_grad}


eps = 1e-05
highest = lax.Precision.HIGHEST

def block_terms(values, keys_in, reads, logdec, user_row, before_user, after_user):
    row_count = values.shape[0]
    head_count = logdec.shape[0]
    cumulative = jnp.cumsum(logdec, axis=1)
    total_log = cumulative[:, -1]
    intersections = jnp.dot(reads, keys_in.T, preferred_element_type=jnp.float32)
    same_user = user_row[:, None] == user_row[None, :]
    spread = cumulative[:, :, None] - cumulative[:, None, :]
    doubled = 1.0 + jnp.eye(row_count, dtype=jnp.float32)
    weights = jnp.where(same_user[None], intersections[None] * doubled[None] * jnp.exp(-jnp.abs(spread)), 0.0).astype(jnp.bfloat16)
    per_head = values.reshape(row_count, head_count, -1)
    inner = jnp.einsum('hts,shp->thp', weights.astype(jnp.float32), per_head.astype(jnp.float32), precision=highest)
    tail_user = (user_row == user_row[-1]).astype(jnp.float32)
    head_user = (user_row == user_row[0]).astype(jnp.float32)
    fwd_scale = (jnp.exp(total_log[:, None] - cumulative) * tail_user[None]).T
    rev_scale = (jnp.exp(cumulative) * head_user[None]).T
    fwd_keys = (keys_in[:, None, :] * fwd_scale[:, :, None]).astype(jnp.bfloat16)
    rev_keys = (keys_in[:, None, :] * rev_scale[:, :, None]).astype(jnp.bfloat16)
    fwd_state = jnp.einsum('shn,shp->hnp', fwd_keys.astype(jnp.float32), per_head.astype(jnp.float32), precision=highest).astype(jnp.bfloat16)
    rev_state = jnp.einsum('shn,shp->hnp', rev_keys.astype(jnp.float32), per_head.astype(jnp.float32), precision=highest).astype(jnp.bfloat16)
    passing = jnp.exp(total_log)
    fwd_gain = (passing * (user_row[-1] == before_user).astype(jnp.float32)).astype(jnp.bfloat16)
    rev_gain = (passing * (user_row[0] == after_user).astype(jnp.float32)).astype(jnp.bfloat16)
    return (inner, cumulative, fwd_gain, fwd_state, rev_gain, rev_state)

def apply_carries(inner, reads, cumulative, user_row, before_user, after_user, from_before, from_after):
    reads_wide = reads.astype(jnp.float32)
    earlier_part = jnp.einsum('tn,hnp->thp', reads_wide, from_before.astype(jnp.float32), precision=highest)
    following_part = jnp.einsum('tn,hnp->thp', reads_wide, from_after.astype(jnp.float32), precision=highest)
    earlier_scale = (jnp.exp(cumulative) * (user_row == before_user).astype(jnp.float32)[None]).T[:, :, None]
    following_scale = (jnp.exp(cumulative[:, -1:] - cumulative) * (user_row == after_user).astype(jnp.float32)[None]).T[:, :, None]
    row_count = inner.shape[0]
    return (inner + earlier_scale * earlier_part + following_scale * following_part).reshape(row_count, -1)

def block_terms_packed(packed):
    return block_terms(*packed)

def apply_packed(packed):
    return apply_carries(*packed)

def advance(running, pair):
    gain_now, state_now = pair
    following = (gain_now.astype(jnp.float32)[:, None, None] * running.astype(jnp.float32) + state_now.astype(jnp.float32)).astype(jnp.bfloat16)
    return (following, running)

def mix(values, keys_in, reads, logdec, user_row):
    block_count = PACKED_OCCASIONS // TOK_DEV
    head_count = logdec.shape[0]
    value_blocks = values.reshape(block_count, TOK_DEV, -1)
    key_blocks = keys_in.reshape(block_count, TOK_DEV, -1)
    read_blocks = reads.reshape(block_count, TOK_DEV, -1)
    log_blocks = logdec.reshape(head_count, block_count, TOK_DEV).transpose(1, 0, 2)
    user_blocks = user_row.reshape(block_count, TOK_DEV)
    padding = jnp.full((1,), -1, jnp.int32)
    before_all = jnp.concatenate([padding, user_blocks[:-1, -1].astype(jnp.int32)])
    after_all = jnp.concatenate([user_blocks[1:, 0].astype(jnp.int32), padding])
    inner, cumulative, fwd_gain, fwd_state, rev_gain, rev_state = lax.map(block_terms_packed, (value_blocks, key_blocks, read_blocks, log_blocks, user_blocks, before_all, after_all))
    empty_state = jnp.zeros(fwd_state.shape[1:], jnp.bfloat16)
    unused_one, from_before = lax.scan(advance, empty_state, (fwd_gain, fwd_state))
    unused_two, from_after = lax.scan(advance, empty_state, (rev_gain, rev_state), reverse=True)
    combined = lax.map(apply_packed, (inner, read_blocks, cumulative, user_blocks, before_all, after_all, from_before, from_after))
    return combined.reshape(PACKED_OCCASIONS, -1)

def reference(features, gate_in, state_in, state_out, step_size, decay_rate, user_ids, norm_gain, out_weight, out_grad):

    def one_sequence(sequence_in):
        values, gates, keys_in, reads, step_row, user_row, grad_local = sequence_in
        logdec = -step_row * decay_rate[:, None]
        mixed_wide = mix(values, keys_in, reads, logdec, user_row)

        def normalize(mixed_rows):
            gated = mixed_rows * jax.nn.silu(gates.astype(jnp.float32))
            multiplier_value = lax.rsqrt(lax.optimization_barrier(jnp.mean(gated * gated, axis=-1, keepdims=True)) + eps)
            return gated * multiplier_value * norm_gain.astype(jnp.float32)
        normed_wide, pullback = jax.vjp(normalize, mixed_wide)
        normed_out = normed_wide.astype(jnp.bfloat16)
        result = jnp.dot(normed_out, out_weight, preferred_element_type=jnp.float32).astype(jnp.bfloat16)
        grad_normed = lax.dot_general(grad_local, out_weight, (((1,), (1,)), ((), ())), preferred_element_type=jnp.float32)
        grad_mixed = pullback(grad_normed)[0].astype(jnp.bfloat16)
        grad_feat = mix(grad_mixed, reads, keys_in, logdec, user_row).astype(jnp.bfloat16)
        return (result, grad_feat, normed_out)
    mixed, feature_grad, normalized = lax.map(one_sequence, (features, gate_in, state_in, state_out, step_size, user_ids, out_grad))
    weight_grad = lax.dot_general(normalized.reshape(-1, INNER), out_grad.reshape(-1, DW), (((0,), (0,)), ((), ())), preferred_element_type=jnp.float32)
    return (mixed, feature_grad, weight_grad)
```

```python
import jax
import jax.numpy as jnp
from jax import lax
from jax.sharding import PartitionSpec as P

eps = 1e-05


def carried_in(gain, state, axis, backward):
    count = lax.axis_size(axis)
    window = count // 2
    sign = -1 if backward else 1

    def shifted(value, distance):
        pairs = [
            (i, i + sign * distance) for i in range(count) if 0 <= i + sign * distance < count
        ]
        return lax.ppermute(value, axis, pairs)

    heads, _, width = state.shape
    distance = 1
    while distance < window:
        row = jnp.broadcast_to(gain[:, None, None], (heads, 8, width))
        far = shifted(jnp.concatenate([state, row], axis=1), distance)
        wide = gain.astype(jnp.float32)
        state = (
            wide[:, None, None] * far[:, :-8].astype(jnp.float32) + state.astype(jnp.float32)
        ).astype(jnp.bfloat16)
        gain = (wide * far[:, -1, 0].astype(jnp.float32)).astype(jnp.bfloat16)
        distance *= 2
    return shifted(state, 1)


def summed_rows(partial, axes):
    sizes = [lax.axis_size(axis) for axis in axes]
    total = 1
    for size in sizes:
        total *= size
    mine = lax.axis_index(axes)
    bits = []
    bit = 1
    while bit < total:
        bits.append(bit)
        bit *= 2
    rows, columns = partial.shape
    held = partial.reshape((2,) * len(bits) + (rows // total, columns))
    for place, bit in enumerate(bits):
        dim = len(bits) - 1 - place
        low = lax.index_in_dim(held, 0, dim, keepdims=False)
        high = lax.index_in_dim(held, 1, dim, keepdims=False)
        upper = (mine // bit) % 2 == 1
        keep = jnp.where(upper, high, low)
        send = jnp.where(upper, low, high).astype(jnp.bfloat16)
        got = lax.ppermute(send, axes, [(i, i ^ bit) for i in range(total)])
        held = keep + got.astype(jnp.float32)
    return held


def padded(x, sides, width):
    for axis, dim in sides:
        size, length = (lax.axis_size(axis), x.shape[dim])
        up = [(i, (i + 1) % size) for i in range(size - 1)]
        down = [(j, i) for i, j in up]
        last = lax.slice_in_dim(x, length - width, length, axis=dim)
        leading = lax.slice_in_dim(x, 0, width, axis=dim)
        before = lax.ppermute(last, axis, up)
        after = lax.ppermute(leading, axis, down)
        x = jnp.concatenate([before, x, after], axis=dim)
    return x


def block_terms(values, keys_in, reads, logdec, user_row, before_user, after_user):
    row_count = values.shape[0]
    head_count = logdec.shape[0]
    cumulative = jnp.cumsum(logdec, axis=1)
    total_log = cumulative[:, -1]
    intersections = jnp.dot(reads, keys_in.T, preferred_element_type=jnp.float32)
    same_user = user_row[:, None] == user_row[None, :]
    spread = cumulative[:, :, None] - cumulative[:, None, :]
    doubled = 1.0 + jnp.eye(row_count, dtype=jnp.float32)
    weights = jnp.where(
        same_user[None], intersections[None] * doubled[None] * jnp.exp(-jnp.abs(spread)), 0.0
    ).astype(jnp.bfloat16)
    per_head = values.reshape(row_count, head_count, -1)
    inner = jnp.einsum("hts,shp->thp", weights, per_head, preferred_element_type=jnp.float32)
    tail_user = (user_row == user_row[-1]).astype(jnp.float32)
    head_user = (user_row == user_row[0]).astype(jnp.float32)
    fwd_scale = (jnp.exp(total_log[:, None] - cumulative) * tail_user[None]).T
    rev_scale = (jnp.exp(cumulative) * head_user[None]).T
    fwd_keys = (keys_in[:, None, :] * fwd_scale[:, :, None]).astype(jnp.bfloat16)
    rev_keys = (keys_in[:, None, :] * rev_scale[:, :, None]).astype(jnp.bfloat16)
    fwd_state = jnp.einsum(
        "shn,shp->hnp", fwd_keys, per_head, preferred_element_type=jnp.float32
    ).astype(jnp.bfloat16)
    rev_state = jnp.einsum(
        "shn,shp->hnp", rev_keys, per_head, preferred_element_type=jnp.float32
    ).astype(jnp.bfloat16)
    passing = jnp.exp(total_log)
    fwd_gain = (passing * (user_row[-1] == before_user).astype(jnp.float32)).astype(jnp.bfloat16)
    rev_gain = (passing * (user_row[0] == after_user).astype(jnp.float32)).astype(jnp.bfloat16)
    return (inner, cumulative, fwd_gain, fwd_state, rev_gain, rev_state)


def apply_carries(
    inner, reads, cumulative, user_row, before_user, after_user, from_before, from_after
):
    earlier_part = jnp.einsum("tn,hnp->thp", reads, from_before, preferred_element_type=jnp.float32)
    following_part = jnp.einsum(
        "tn,hnp->thp", reads, from_after, preferred_element_type=jnp.float32
    )
    earlier_scale = (jnp.exp(cumulative) * (user_row == before_user).astype(jnp.float32)[None]).T[
        :, :, None
    ]
    following_scale = (
        jnp.exp(cumulative[:, -1:] - cumulative)
        * (user_row == after_user).astype(jnp.float32)[None]
    ).T[:, :, None]
    row_count = inner.shape[0]
    return (inner + earlier_scale * earlier_part + following_scale * following_part).reshape(
        row_count, -1
    )


def mix_local(values, keys_in, reads, logdec, user_row, before_user, after_user):
    inner, cumulative, fwd_gain, fwd_state, rev_gain, rev_state = block_terms(
        values, keys_in, reads, logdec, user_row, before_user, after_user
    )
    from_before = carried_in(fwd_gain, fwd_state, "ctx", False)
    from_after = carried_in(rev_gain, rev_state, "ctx", True)
    return apply_carries(
        inner, reads, cumulative, user_row, before_user, after_user, from_before, from_after
    )


def local(
    features,
    gate_in,
    state_in,
    state_out,
    step_size,
    decay_rate,
    user_ids,
    norm_gain,
    out_weight,
    out_grad,
):
    neighbours = padded(user_ids + 1, (("ctx", 1),), 1) - 1
    user_row = user_ids[0]
    before_user = neighbours[0, 0]
    after_user = neighbours[0, -1]
    logdec = -step_size[0] * decay_rate[:, None]
    values = features[0]
    gates = gate_in[0]
    keys_in = state_in[0]
    reads = state_out[0]
    grad_local = out_grad[0]
    mixed_wide = mix_local(values, keys_in, reads, logdec, user_row, before_user, after_user)

    def normalize(mixed_rows):
        gated = mixed_rows * jax.nn.silu(gates.astype(jnp.float32))
        multiplier_value = lax.rsqrt(jnp.mean(gated * gated, axis=-1, keepdims=True) + eps)
        return gated * multiplier_value * norm_gain.astype(jnp.float32)

    normed_wide, pullback = jax.vjp(normalize, mixed_wide)
    normed_out = normed_wide.astype(jnp.bfloat16)
    full_weight = lax.all_gather(out_weight, ("dp", "ctx"), axis=0, tiled=True)
    result = jnp.dot(normed_out, full_weight, preferred_element_type=jnp.float32)
    grad_normed = lax.dot_general(
        grad_local, full_weight, (((1,), (1,)), ((), ())), preferred_element_type=jnp.float32
    )
    grad_mixed = pullback(grad_normed)[0].astype(jnp.bfloat16)
    grad_feat = mix_local(grad_mixed, reads, keys_in, logdec, user_row, before_user, after_user)
    weight_grad = summed_rows(
        lax.dot_general(
            normed_out, grad_local, (((0,), (0,)), ((), ())), preferred_element_type=jnp.float32
        ),
        ("dp", "ctx"),
    )
    return (result.astype(jnp.bfloat16)[None], grad_feat.astype(jnp.bfloat16)[None], weight_grad)


def solution(mesh):
    placed = (
        P("dp", "ctx", None),
        P("dp", "ctx", None),
        P("dp", "ctx", None),
        P("dp", "ctx", None),
        P("dp", None, "ctx"),
        P(),
        P("dp", "ctx"),
        P(),
        P(("dp", "ctx"), None),
        P("dp", "ctx", None),
    )
    return jax.shard_map(
        local,
        mesh=mesh,
        in_specs=placed,
        out_specs=(P("dp", "ctx", None), P("dp", "ctx", None), P(("dp", "ctx"), None)),
        check_vma=False,
    )
```
